32 devices in a mesh: dp: 8 (over z, y), tensor: 4 (over x, core).
Axes of the slice: x: 2, y: 2, z: 4, core: 2. Of those that a mesh axis runs over, the one named last changes fastest.
Arguments:
- tokens: bfloat16 [512, 1536], P('dp'), may hold values from -6 to 6
- norm_gain: float32 [1536], replicated, may hold values from 0.1 to 1.9
- w_query: bfloat16 [1536, 1024], P(None, 'tensor'), may hold values from -0.15625 to 0.15625
- w_keyval: bfloat16 [1536, 256], replicated, may hold values from -0.15625 to 0.15625
- w_out: bfloat16 [1024, 1536], P('tensor'), may hold values from -0.5 to 0.5
- kv_pool: bfloat16 [4096, 128, 256], P(('dp', 'tensor')), may hold values from -256 to 256
- page_table: int32 [512, 8], P('dp', 'tensor'), may hold values from 0 to 127, as said below
- positions: int32 [512], P('dp'), may hold values from 0 to 8191
- assignment: int32 [512], P('dp'), may hold values from 0 to 511, as said below
Outputs:
- attn_out: bfloat16 [512, 1536], P('dp')
The draws below stay inside these ranges and needn't reach their ends.
Inputs may be any that keep to these rules, and one draw needn't show every extreme that they name: `assignment`: the serving slot is the serving device's dp index times 64 plus a local slot; each serving slot is taken by exactly one request; the 64 requests of one device go to 8 distinct devices, exactly 8 to each. `page_table`: on each device the entries form a permutation of 0 to 127.
All inputs are finite; a program needn't handle non-finite values.
Results may differ from the reference program's by a relative error of at most 0.03.
Values may be sent and summed in bfloat16 or wider, within the bound.
A program may use at most 64 MiB of HBM per device.

```python
import math
import jax
import jax.numpy as jnp
from jax import lax

D = 1536
HEADS = 8
HD = 128
WINDOW = 1024
PAGE = 128
R_DEV = 64
CYCLE = 8
PPD = 2
POOL_DEV = 128
CAP = 8
REQ = 512
N_DP = 8
N_TENSOR = 4


def draw_kv_pool(key, part):
    first_key = jax.random.fold_in(key, 0)
    shape = (N_DP * N_TENSOR * POOL_DEV, PAGE, 2 * HD)
    base = jnp.clip(jax.random.normal(first_key, shape, jnp.float32), -4.0, 4.0)
    keys_part = base[..., :HD] * 2.0
    values_part = base[..., HD:]
    return jnp.concatenate([keys_part, values_part], axis=-1).astype(jnp.bfloat16)


def draw_page_table(key, part):
    subkeys = jax.random.split(key, N_DP * N_TENSOR)
    perms = jax.vmap(lambda k: jax.random.permutation(k, POOL_DEV))(subkeys)
    perms = perms.reshape(N_DP, N_TENSOR, R_DEV, PPD).transpose(0, 2, 1, 3)
    return perms.reshape(N_DP * R_DEV, N_TENSOR * PPD).astype(jnp.int32)


def draw_positions(key, part):
    first_key, second_key, third_key, fourth_key = jax.random.split(key, 4)
    highest = int(math.log2(WINDOW)) + 3
    powers = jax.random.randint(first_key, (REQ,), 3, highest + 1)
    limits = jnp.left_shift(jnp.ones((REQ,), jnp.int32), powers)
    drawn = jax.random.randint(second_key, (REQ,), 0, limits).astype(jnp.int32)
    top_index = jax.random.randint(third_key, (), 0, REQ)
    low_index = (top_index + 1 + jax.random.randint(fourth_key, (), 0, REQ - 1)) % REQ
    drawn = drawn.at[top_index].set(8 * WINDOW - 1)
    drawn = drawn.at[low_index].set(0)
    return drawn.astype(jnp.int32)


def draw_assignment(key, part):
    first_key, second_key, third_key = jax.random.split(key, 3)
    groups = R_DEV // CAP
    offsets = jax.random.permutation(first_key, N_DP)[:groups]
    ranks = jax.vmap(lambda k: jax.random.permutation(k, R_DEV))(jax.random.split(second_key, N_DP))
    sigma = jax.vmap(lambda k: jax.random.permutation(k, R_DEV))(jax.random.split(third_key, N_DP))
    homes = jnp.arange(N_DP)[:, None]
    group_of = ranks // CAP
    within = ranks % CAP
    target = (homes + offsets[group_of]) % N_DP
    local = sigma[target, group_of * CAP + within]
    return (target * R_DEV + local).reshape(-1).astype(jnp.int32)


def shard_levels(stream_key, shape, shards, smallest, high):
    factor_of = 1.0
    for position, parts in shards:
        heights = jax.random.uniform(jax.random.fold_in(jax.random.fold_in(stream_key, 6), position), (parts,), jnp.float32, smallest / len(shards), high / len(shards))
        factor_of = factor_of * jnp.repeat(jnp.exp(heights), shape[position] // parts).reshape((-1,) + (1,) * (len(shape) - 1 - position))
    return factor_of


def centred(stream_key, dims, scale, reach, cuts=(), held_as=jnp.bfloat16):
    factor_of = shard_levels(stream_key, dims, cuts, -0.22, 0.18) if cuts else 1.0
    values = jax.random.normal(stream_key, dims, jnp.float32) * scale * factor_of
    return jnp.minimum(jnp.maximum(values, -reach), reach).astype(held_as)


def setup_inputs(seed: int = 0) -> dict:
    keys = jax.random.split(jax.random.key(seed), 10)
    tokens = centred(keys[0], (REQ, D), 1.0, 6.0, ((0, 8),))
    norm_gain = jnp.clip(1.0 + 0.18 * jax.random.normal(keys[1], (D,), jnp.float32), 0.1, 1.9)
    w_query = centred(keys[2], (D, HEADS * HD), D ** -0.5, 0.15625, ((1, 4),))
    w_keyval = centred(keys[3], (D, 2 * HD), D ** -0.5, 0.15625)
    w_out = centred(keys[4], (HEADS * HD, D), HD ** -0.5, 0.5, ((0, 4),))
    kv_pool = draw_kv_pool(jax.random.fold_in(keys[9], 71), 0)
    page_table = draw_page_table(jax.random.fold_in(keys[9], 71), 0)
    positions = draw_positions(jax.random.fold_in(keys[9], 71), 0)
    assignment = draw_assignment(jax.random.fold_in(keys[9], 71), 0)
    return dict(tokens=tokens, norm_gain=norm_gain, w_query=w_query, w_keyval=w_keyval, w_out=w_out, kv_pool=kv_pool, page_table=page_table, positions=positions, assignment=assignment)


def rotate(values, where, width):
    half = width // 2
    freqs = 10000.0 ** (-jnp.arange(half, dtype=jnp.float32) * 2.0 / width)
    angles = where.astype(jnp.float32)[..., None] * freqs
    cosine = jnp.cos(angles)
    sine = jnp.sin(angles)
    first = values[..., :half]
    second = values[..., half:]
    return jnp.concatenate([first * cosine - second * sine, first * sine + second * cosine], axis=-1)

def reference(tokens, norm_gain, w_query, w_keyval, w_out, kv_pool, page_table, positions, assignment):
    floats = tokens.astype(jnp.float32)
    normed = (floats * lax.rsqrt(lax.optimization_barrier(jnp.mean(floats * floats, axis=-1, keepdims=True)) + 1e-06) * norm_gain).astype(jnp.bfloat16)
    query = jnp.dot(normed, w_query, preferred_element_type=jnp.float32).reshape(REQ, HEADS, HD)
    query = rotate(query, positions[:, None], HD).astype(jnp.bfloat16)
    key_value = jnp.dot(normed, w_keyval, preferred_element_type=jnp.float32)
    new_key = rotate(key_value[:, :HD], positions, HD).astype(jnp.bfloat16)
    new_value = key_value[:, HD:].astype(jnp.bfloat16)
    serve_dev = (assignment // R_DEV).astype(jnp.int32)
    table = page_table[assignment]
    owner = (jnp.arange(CYCLE) // PPD).astype(jnp.int32)
    global_page = ((serve_dev[:, None] * N_TENSOR + owner[None, :]) * POOL_DEV + table).astype(jnp.int32)
    scale = HD ** (-0.5)

    def block(pieces):
        q_block, k_block, v_block, p_block, g_block = pieces
        page_entries = kv_pool[g_block].reshape(R_DEV, WINDOW, 2 * HD).astype(jnp.float32)
        q_float = q_block.astype(jnp.float32)
        scores = jnp.einsum('rhd,rkd->rhk', q_float, page_entries[..., :HD]) * scale
        own = jnp.einsum('rhd,rd->rh', q_float, k_block.astype(jnp.float32)) * scale
        offset = jnp.mod(jnp.arange(WINDOW, dtype=jnp.int32)[None, :] - p_block[:, None], WINDOW)
        valid = (offset != 0) & (p_block[:, None] - WINDOW + offset >= 0)
        scores = jnp.where(valid[:, None, :], scores, -jnp.inf)
        top = jnp.maximum(lax.optimization_barrier(jnp.max(scores, axis=2)), own)
        weight_tensors = jnp.exp(scores - top[..., None])
        own_weight = jnp.exp(own - top)
        total = lax.optimization_barrier(jnp.sum(weight_tensors, axis=2)) + own_weight
        weights_low = lax.optimization_barrier(weight_tensors.astype(jnp.bfloat16)).astype(jnp.float32)
        local_lower_index = lax.optimization_barrier(own_weight.astype(jnp.bfloat16)).astype(jnp.float32)
        summed = jnp.einsum('rhk,rkd->rhd', weights_low, page_entries[..., HD:])
        summed = summed + local_lower_index[..., None] * v_block.astype(jnp.float32)[:, None, :]
        return (summed / total[..., None]).astype(jnp.bfloat16)
    attended = lax.map(block, (query.reshape(N_DP, R_DEV, HEADS, HD), new_key.reshape(N_DP, R_DEV, HD), new_value.reshape(N_DP, R_DEV, HD), positions.reshape(N_DP, R_DEV), global_page.reshape(N_DP, R_DEV, CYCLE)))
    attended = attended.reshape(REQ, HEADS * HD)
    return jnp.dot(attended, w_out, preferred_element_type=jnp.float32).astype(jnp.bfloat16)
```

```python
import functools

import jax
import jax.numpy as jnp
from jax import lax
from jax.experimental import pallas as pl
from jax.experimental.pallas import tpu as pltpu
from jax.sharding import PartitionSpec as P

masked_score = -1e30
peak_floor = -1e29
norm_eps = 1e-06
rotary_base = 10000.0
chunks = 8
MESH = pl.DeviceIdType.MESH
f32 = jnp.float32
bf16 = jnp.bfloat16


def dot(a, b):
    return jnp.dot(a, b, preferred_element_type=f32)


def dot_t(a, b):
    return lax.dot_general(a, b, (((1,), (1,)), ((), ())), preferred_element_type=f32)


def dot_exact(a, b):
    return jnp.dot(a, b, preferred_element_type=f32, precision=lax.Precision.HIGHEST)


def iota(shape, axis):
    return lax.broadcasted_iota(jnp.int32, shape, axis)


def split(values):
    high = values.astype(bf16).astype(f32)
    rest = values - high
    middle = rest.astype(bf16).astype(f32)
    return high, middle, rest - middle


def kernel(
    n_dp,
    n_tensor,
    capacity,
    tokens_hbm,
    gain_ref,
    wq_hbm,
    wkv_hbm,
    wo_hbm,
    pool_hbm,
    table_ref,
    position_ref,
    assign_ref,
    freq_ref,
    out_ref,
    tokens,
    wq,
    wkv,
    wo,
    pool,
    q_out,
    meta_out,
    q_in,
    meta_in,
    page_q,
    page_s,
    page_acc,
    stat_out,
    stat_in,
    sum_out,
    sum_in,
    load_sem,
    pool_sem,
    send_sem,
    recv_sem,
):
    dp = lax.axis_index("dp")
    tp = lax.axis_index("tensor")
    n_all = n_dp * n_tensor
    me = tp * n_dp + dp
    rows = tokens.shape[0]
    slots = n_dp * capacity
    width = wkv.shape[1] // 2
    half = width // 2
    local_heads = wq.shape[1] // width
    heads = local_heads * n_tensor
    pages, page_len = pool.shape[0], pool.shape[1]
    page_rows = table_ref.shape[1]
    window = page_rows * n_tensor * page_len
    chunk = pages // chunks
    scale = width ** (-0.5)
    out_rows = rows // n_tensor

    loads = [
        pltpu.make_async_copy(src, dst, load_sem.at[i])
        for i, (src, dst) in enumerate(
            ((tokens_hbm, tokens), (wq_hbm, wq), (wkv_hbm, wkv), (wo_hbm, wo))
        )
    ]
    for load in loads[:2]:
        load.start()

    barrier = pltpu.get_barrier_semaphore()

    def peer_of(i):
        other = lax.rem(me + i, n_all)
        return lax.rem(other, n_dp), lax.div(other, n_dp)

    @pl.loop(1, n_all)
    def _(i):
        pl.semaphore_signal(barrier, inc=1, device_id=peer_of(i), device_id_type=MESH)

    for load in loads[2:]:
        load.start()

    def pool_load(i):
        part = pl.ds(i * chunk, chunk)
        return pltpu.make_async_copy(pool_hbm.at[part], pool.at[part], pool_sem.at[i])

    for i in range(chunks):
        pool_load(i).start()

    eye = iota((rows, rows), 0) == iota((rows, rows), 1)
    before = iota((rows, rows), 1) < iota((rows, rows), 0)
    after = iota((rows, rows), 1) > iota((rows, rows), 0)

    def as_column(row):
        return jnp.sum(jnp.where(eye, row, 0.0), axis=1, keepdims=True)

    def as_row(column):
        return jnp.sum(jnp.where(eye, column, 0.0), axis=0, keepdims=True)

    position_row = position_ref[...].astype(f32)
    position = as_column(position_row)
    target_int = lax.div(assign_ref[...], rows)
    slot_row = (assign_ref[...] - target_int * rows).astype(f32)
    target_row = target_int.astype(f32)
    target = as_column(target_row)
    same = (target == target_row).astype(f32)
    place_row = target_row * capacity + jnp.sum(
        jnp.where(after, same, 0.0), axis=0, keepdims=True
    )
    place = target * capacity + jnp.sum(jnp.where(before, same, 0.0), axis=1, keepdims=True)
    to_place = iota((slots, rows), 0).astype(f32) == place_row
    from_place = (iota((rows, slots), 1).astype(f32) == place).astype(bf16)
    routed = to_place.astype(bf16)
    sent_position = jnp.sum(jnp.where(to_place, position_row, 0.0), axis=1, keepdims=True)
    sent_slot = jnp.sum(jnp.where(to_place, slot_row + 1.0, 0.0), axis=1, keepdims=True)
    high = jnp.floor(sent_position * (1.0 / 128.0))
    low = sent_position - high * 128.0
    lane = iota((slots, 128), 1)
    meta = jnp.where(lane == 0, high, jnp.where(lane == 1, low, jnp.where(lane == 2, sent_slot, 0.0)))
    meta_out[...] = meta.reshape(n_dp, capacity, 128).astype(bf16)

    angles = position * freq_ref[...]
    cosine = jnp.cos(angles)
    sine = jnp.sin(angles)

    def rotate(values):
        first, second = values[:, :half], values[:, half:]
        return jnp.concatenate(
            [first * cosine - second * sine, first * sine + second * cosine], axis=1
        )

    loads[0].wait()
    floats = tokens[...].astype(f32)
    normed = (
        floats
        * lax.rsqrt(jnp.mean(floats * floats, axis=-1, keepdims=True) + norm_eps)
        * gain_ref[...]
    ).astype(bf16)
    loads[1].wait()
    raw = dot(normed, wq[...])
    query = jnp.concatenate(
        [rotate(raw[:, h * width : (h + 1) * width]) for h in range(local_heads)], axis=1
    ).astype(bf16)
    q_out[...] = dot(routed, query).reshape(n_dp, capacity, local_heads * width).astype(bf16)

    pl.semaphore_wait(barrier, n_all - 1)

    def remote(src, dst, k, where):
        return pltpu.make_async_remote_copy(
            src_ref=src,
            dst_ref=dst,
            send_sem=send_sem.at[k],
            recv_sem=recv_sem.at[k],
            device_id=where,
            device_id_type=MESH,
        )

    def local_copy(src, dst, k):
        return pltpu.make_async_copy(src, dst, recv_sem.at[k])

    def wait_for(ref, sem):
        pltpu.make_async_copy(ref, ref, sem).wait()

    @pl.loop(1, n_dp)
    def _(i):
        d = lax.rem(dp + i, n_dp)
        remote(meta_out.at[d], meta_in.at[dp], 0, (d, tp)).start()

    local_copy(meta_out.at[dp], meta_in.at[dp], 0).start()

    @pl.loop(1, n_all)
    def _(i):
        d, t = peer_of(i)
        remote(q_out.at[d], q_in.at[me], 1, (d, t)).start()

    local_copy(q_out.at[dp], q_in.at[me], 1).start()

    loads[2].wait()
    key_value = dot(normed, wkv[...])
    new_key = rotate(key_value[:, :width]).astype(bf16).astype(f32)
    new_value = key_value[:, width:].astype(bf16).astype(f32)
    self_scores = [
        jnp.sum(
            query[:, h * width : (h + 1) * width].astype(f32) * new_key, axis=1, keepdims=True
        )
        * scale
        for h in range(local_heads)
    ]

    table = table_ref[...].astype(f32)
    page_id = iota((pages, rows), 0).astype(f32)
    holds = [(page_id == as_row(table[:, j : j + 1])).astype(f32) for j in range(page_rows)]
    first_page = holds[0].astype(bf16)
    any_page = sum(holds).astype(bf16)
    which = sum(j * jnp.sum(holds[j], axis=1, keepdims=True) for j in range(page_rows))
    swap = dot_t(any_page, any_page)
    swap = jnp.where(iota((pages, pages), 0) == iota((pages, pages), 1), 0.0, swap)
    key_slot = (tp * page_rows * page_len).astype(f32) + which * page_len + iota(
        (pages, page_len), 1
    ).astype(f32)

    wait_for(meta_in, recv_sem.at[0])
    got = meta_in[...].astype(f32).reshape(slots, 128)
    serves = (got[:, 2:3] - 1.0 == iota((slots, rows), 1).astype(f32)).astype(bf16)
    to_page = dot_t(any_page, serves).astype(bf16)
    from_page = dot_t(serves, any_page).astype(bf16)
    from_first = dot_t(serves, first_page)
    page_meta = dot(to_page, got.astype(bf16))
    page_position = page_meta[:, 0:1] * 128.0 + page_meta[:, 1:2]
    gap = key_slot - page_position
    offset = gap - window * jnp.floor(gap * (1.0 / window))
    live = (offset != 0.0) & (page_position - window + offset >= 0.0)
    mask = jnp.where(live, 0.0, masked_score)

    wait_for(q_in, recv_sem.at[1])
    for t in range(n_tensor):
        part = q_in[t * n_dp : (t + 1) * n_dp].astype(f32).reshape(slots, local_heads * width)
        spread = dot(to_page, part.astype(bf16))
        for h in range(local_heads):
            page_q[pl.ds(t * local_heads + h, pages, stride=heads), :] = spread[
                :, h * width : (h + 1) * width
            ]

    for i in range(chunks):
        pool_load(i).wait()

    pairs = pages // 2
    unroll = 8

    @pl.loop(0, pairs // unroll)
    def _(step):
        for u in range(unroll):
            pair = step * unroll + u
            at = pl.multiple_of(pair * 2 * heads, 2 * heads)
            keys = pool[pl.ds(pair * 2, 2), :, :width].reshape(2 * page_len, width)
            scores = dot_t(page_q[pl.ds(at, 2 * heads), :].astype(bf16), keys)
            page_s[pl.ds(at, heads), :] = scores[:heads, :page_len]
            page_s[pl.ds(at + heads, heads), :] = scores[heads:, page_len:]

    lanes = lax.rem(iota((pages, 128), 1), heads)
    peaks = jnp.zeros((pages, 128), f32)
    for h in range(heads):
        scored = page_s[pl.ds(h, pages, stride=heads), :] * scale + mask
        top = jnp.max(scored, axis=1, keepdims=True)
        peaks = jnp.where(lanes == h, top, peaks)
    peaks = jnp.maximum(peaks, peak_floor)
    peaks = jnp.maximum(peaks, dot_exact(swap, peaks))
    totals = jnp.zeros((pages, 128), f32)
    for h in range(heads):
        scored = page_s[pl.ds(h, pages, stride=heads), :] * scale + mask
        weight = jnp.exp(scored - peaks[:, h : h + 1])
        totals = jnp.where(lanes == h, jnp.sum(weight, axis=1, keepdims=True), totals)
        page_s[pl.ds(h, pages, stride=heads), :] = weight

    upper = iota((2 * heads, page_len), 0) < heads

    @pl.loop(0, pairs // unroll)
    def _(step):
        for u in range(unroll):
            pair = step * unroll + u
            at = pl.multiple_of(pair * 2 * heads, 2 * heads)
            weight = page_s[pl.ds(at, 2 * heads), :]
            both = jnp.concatenate(
                [jnp.where(upper, weight, 0.0), jnp.where(upper, 0.0, weight)], axis=1
            ).astype(bf16)
            values = pool[pl.ds(pair * 2, 2), :, width:].reshape(2 * page_len, width)
            page_acc[pl.ds(at, 2 * heads), :] = dot(both, values)

    own_peak = split(dot_exact(from_first, peaks))
    own_total = split(dot_exact(from_page.astype(f32), totals))
    group = lax.div(iota((slots, 128), 1), heads)
    stats = jnp.zeros((slots, 128), f32)
    for k, piece in enumerate(own_peak + own_total):
        stats = jnp.where(group == k, piece, stats)
    stats = stats.reshape(n_dp, capacity, 128).astype(bf16)
    for t in range(n_tensor):
        for h in range(local_heads):
            summed = page_acc[pl.ds(t * local_heads + h, pages, stride=heads), :].astype(bf16)
            stat_out[t * n_dp : (t + 1) * n_dp, :, h * width : (h + 1) * width] = (
                dot(from_page, summed).reshape(n_dp, capacity, width).astype(bf16)
            )
        stat_out[t * n_dp : (t + 1) * n_dp, :, local_heads * width :] = stats

    @pl.loop(1, n_all)
    def _(i):
        d, t = peer_of(i)
        remote(stat_out.at[t * n_dp + d], stat_in.at[me], 2, (d, t)).start()

    local_copy(stat_out.at[me], stat_in.at[me], 2).start()

    loads[3].wait()
    wait_for(stat_in, recv_sem.at[2])
    parts = []
    for t in range(n_tensor):
        part = stat_in[t * n_dp : (t + 1) * n_dp].astype(f32).reshape(slots, stat_in.shape[2])
        parts.append(dot(from_place, part.astype(bf16)))
    row_lane = iota((rows, 128), 1)
    row_head = lax.rem(row_lane, heads)
    row_group = lax.div(row_lane, heads)
    attended = []
    for h in range(local_heads):
        mine = row_head == tp * local_heads + h
        is_peak = mine & (row_group < 3)
        is_total = mine & (row_group >= 3) & (row_group < 6)
        tops, sums = [], []
        for part in parts:
            stat = part[:, local_heads * width :]
            tops.append(jnp.sum(jnp.where(is_peak, stat, 0.0), axis=1, keepdims=True))
            sums.append(jnp.sum(jnp.where(is_total, stat, 0.0), axis=1, keepdims=True))
        overall = functools.reduce(jnp.maximum, tops, self_scores[h])
        fresh = jnp.exp(self_scores[h] - overall)
        total = fresh
        acc = fresh.astype(bf16).astype(f32) * new_value
        for top, add, part in zip(tops, sums, parts):
            keep = jnp.exp(top - overall)
            total = total + add * keep
            acc = acc + part[:, h * width : (h + 1) * width] * keep
        attended.append(acc / total)
    attended = jnp.concatenate(attended, axis=1).astype(bf16)
    partial = dot(attended, wo[...])
    sum_out[...] = partial.reshape(n_tensor, out_rows, partial.shape[1]).astype(bf16)

    @pl.loop(1, n_tensor)
    def _(i):
        t = lax.rem(tp + i, n_tensor)
        remote(sum_out.at[t], sum_in.at[tp], 3, (dp, t)).start()

    local_copy(sum_out.at[tp], sum_in.at[tp], 3).start()
    wait_for(sum_in, recv_sem.at[3])
    done = sum_in[0].astype(f32)
    for t in range(1, n_tensor):
        done = done + sum_in[t].astype(f32)
    out_ref[tp] = done.astype(bf16)

    @pl.loop(1, n_tensor)
    def _(i):
        t = lax.rem(tp + i, n_tensor)
        remote(out_ref.at[tp], out_ref.at[tp], 4, (dp, t)).start()

    wait_for(out_ref.at[pl.ds(0, n_tensor - 1)], recv_sem.at[4])
    wait_for(meta_in.at[pl.ds(0, n_dp - 1)], send_sem.at[0])
    wait_for(q_in.at[pl.ds(0, n_all - 1)], send_sem.at[1])
    wait_for(stat_in.at[pl.ds(0, n_all - 1)], send_sem.at[2])
    wait_for(sum_in.at[pl.ds(0, n_tensor - 1)], send_sem.at[3])
    wait_for(out_ref.at[pl.ds(0, n_tensor - 1)], send_sem.at[4])


def local(tokens, norm_gain, w_query, w_keyval, w_out, kv_pool, page_table, positions, assignment):
    n_dp, n_tensor = lax.axis_size("dp"), lax.axis_size("tensor")
    rows, model = tokens.shape
    width = w_keyval.shape[1] // 2
    query_width = w_query.shape[1]
    heads = query_width // width * n_tensor
    capacity = max(8, rows // n_dp)
    n_all = n_dp * n_tensor
    pages = kv_pool.shape[0]
    half = width // 2
    freqs = rotary_base ** (-jnp.arange(half, dtype=f32) * 2.0 / width)
    whole = pl.BlockSpec(memory_space=pltpu.VMEM)
    anywhere = pl.BlockSpec(memory_space=pl.ANY)
    out = pl.pallas_call(
        functools.partial(kernel, n_dp, n_tensor, capacity),
        out_shape=jax.ShapeDtypeStruct((n_tensor, rows // n_tensor, model), bf16),
        in_specs=[anywhere, whole] + [anywhere] * 4 + [whole] * 4,
        out_specs=whole,
        scratch_shapes=[
            pltpu.VMEM(tokens.shape, bf16),
            pltpu.VMEM(w_query.shape, bf16),
            pltpu.VMEM(w_keyval.shape, bf16),
            pltpu.VMEM(w_out.shape, bf16),
            pltpu.VMEM(kv_pool.shape, bf16),
            pltpu.VMEM((n_dp, capacity, query_width), bf16),
            pltpu.VMEM((n_dp, capacity, 128), bf16),
            pltpu.VMEM((n_all, capacity, query_width), bf16),
            pltpu.VMEM((n_dp, capacity, 128), bf16),
            pltpu.VMEM((pages * heads, width), f32),
            pltpu.VMEM((pages * heads, kv_pool.shape[1]), f32),
            pltpu.VMEM((pages * heads, width), f32),
            pltpu.VMEM((n_all, capacity, query_width + 128), bf16),
            pltpu.VMEM((n_all, capacity, query_width + 128), bf16),
            pltpu.VMEM((n_tensor, rows // n_tensor, model), bf16),
            pltpu.VMEM((n_tensor, rows // n_tensor, model), bf16),
            pltpu.SemaphoreType.DMA((4,)),
            pltpu.SemaphoreType.DMA((chunks,)),
            pltpu.SemaphoreType.DMA((5,)),
            pltpu.SemaphoreType.DMA((5,)),
        ],
        compiler_params=pltpu.CompilerParams(
            collective_id=0, has_side_effects=True, vmem_limit_bytes=48 << 20
        ),
    )(
        tokens,
        norm_gain.reshape(1, model),
        w_query,
        w_keyval,
        w_out,
        kv_pool,
        page_table,
        positions.reshape(1, rows),
        assignment.reshape(1, rows),
        freqs.reshape(1, half),
    )
    return out.reshape(rows, model)


def solution(mesh):
    return jax.shard_map(
        local,
        mesh=mesh,
        in_specs=(
            P("dp", None),
            P(),
            P(None, "tensor"),
            P(),
            P("tensor", None),
            P(("dp", "tensor"), None, None),
            P("dp", "tensor"),
            P("dp"),
            P("dp"),
        ),
        out_specs=P("dp", None),
        check_vma=False,
    )
```

```python
import functools
import math

import jax
import jax.numpy as jnp
from jax import lax
from jax.experimental import pallas as pl
from jax.experimental.pallas import tpu as pltpu
from jax.sharding import PartitionSpec as P

masked_score = -1e30
peak_floor = -1e29
norm_eps = 1e-06
rotary_base = 10000.0
chunks = 8
MESH = pl.DeviceIdType.MESH
f32 = jnp.float32
bf16 = jnp.bfloat16


def dot(a, b):
    return jnp.dot(a, b, preferred_element_type=f32)


def dot_t(a, b):
    return lax.dot_general(a, b, (((1,), (1,)), ((), ())), preferred_element_type=f32)


def dot_exact(a, b):
    return jnp.dot(a, b, preferred_element_type=f32, precision=lax.Precision.HIGHEST)


def iota(shape, axis):
    return lax.broadcasted_iota(jnp.int32, shape, axis)


def split(values):
    high = values.astype(bf16).astype(f32)
    rest = values - high
    middle = rest.astype(bf16).astype(f32)
    return high, middle, rest - middle


def kernel(
    n_dp,
    n_tensor,
    capacity,
    tokens_hbm,
    gain_hbm,
    wq_hbm,
    wkv_hbm,
    wo_hbm,
    pool_hbm,
    table_hbm,
    position_hbm,
    assign_hbm,
    out_ref,
    tokens,
    gain_ref,
    table_ref,
    position_ref,
    assign_ref,
    wq,
    wkv,
    wo,
    pool,
    q_out,
    meta_out,
    q_in,
    meta_in,
    page_q,
    page_s,
    page_acc,
    stat_out,
    stat_in,
    sum_out,
    sum_in,
    load_sem,
    pool_sem,
    send_sem,
    recv_sem,
):
    dp = lax.axis_index("dp")
    tp = lax.axis_index("tensor")
    n_all = n_dp * n_tensor
    me = tp * n_dp + dp
    rows = tokens.shape[0]
    slots = n_dp * capacity
    width = wkv.shape[1] // 2
    half = width // 2
    local_heads = wq.shape[1] // width
    heads = local_heads * n_tensor
    pages, page_len = pool.shape[0], pool.shape[1]
    page_rows = table_ref.shape[0]
    window = page_rows * n_tensor * page_len
    chunk = pages // chunks
    scale = width ** (-0.5)
    out_rows = rows // n_tensor

    loads = [
        pltpu.make_async_copy(src, dst, load_sem.at[i])
        for i, (src, dst) in enumerate(
            (
                (position_hbm, position_ref),
                (assign_hbm, assign_ref),
                (tokens_hbm, tokens),
                (gain_hbm, gain_ref),
                (wq_hbm, wq),
                (table_hbm, table_ref),
                (wkv_hbm, wkv),
                (wo_hbm, wo),
            )
        )
    ]
    for load in loads[:5]:
        load.start()

    barrier = pltpu.get_barrier_semaphore()

    def peer_of(i):
        other = lax.rem(me + i, n_all)
        return lax.rem(other, n_dp), lax.div(other, n_dp)

    @pl.loop(1, n_all)
    def _(i):
        pl.semaphore_signal(barrier, inc=1, device_id=peer_of(i), device_id_type=MESH)

    for load in loads[5:]:
        load.start()

    def pool_load(i):
        part = pl.ds(i * chunk, chunk)
        return pltpu.make_async_copy(pool_hbm.at[part], pool.at[part], pool_sem.at[i])

    for i in range(chunks):
        pool_load(i).start()

    eye = iota((rows, rows), 0) == iota((rows, rows), 1)
    before = iota((rows, rows), 1) < iota((rows, rows), 0)
    after = iota((rows, rows), 1) > iota((rows, rows), 0)

    def as_column(row):
        return jnp.sum(jnp.where(eye, row, 0.0), axis=1, keepdims=True)

    loads[0].wait()
    loads[1].wait()
    position_row = position_ref[...].astype(f32)
    position = as_column(position_row)
    target_int = lax.div(assign_ref[...], rows)
    slot_row = (assign_ref[...] - target_int * rows).astype(f32)
    target_row = target_int.astype(f32)
    target = as_column(target_row)
    same = (target == target_row).astype(f32)
    place_row = target_row * capacity + jnp.sum(
        jnp.where(after, same, 0.0), axis=0, keepdims=True
    )
    place = target * capacity + jnp.sum(jnp.where(before, same, 0.0), axis=1, keepdims=True)
    to_place = iota((slots, rows), 0).astype(f32) == place_row
    from_place = (iota((rows, slots), 1).astype(f32) == place).astype(bf16)
    routed = to_place.astype(bf16)
    sent_position = jnp.sum(jnp.where(to_place, position_row, 0.0), axis=1, keepdims=True)
    sent_slot = jnp.sum(jnp.where(to_place, slot_row + 1.0, 0.0), axis=1, keepdims=True)
    high = jnp.floor(sent_position * (1.0 / 128.0))
    low = sent_position - high * 128.0
    lane = iota((slots, 128), 1)
    meta = jnp.where(lane == 0, high, jnp.where(lane == 1, low, jnp.where(lane == 2, sent_slot, 0.0)))
    meta_out[...] = meta.reshape(n_dp, capacity, 128).astype(bf16)

    step = -2.0 * math.log(rotary_base) / width
    angles = position * jnp.exp(iota((1, half), 1).astype(f32) * step)
    cosine = jnp.cos(angles)
    sine = jnp.sin(angles)

    def rotate(values):
        first, second = values[:, :half], values[:, half:]
        return jnp.concatenate(
            [first * cosine - second * sine, first * sine + second * cosine], axis=1
        )

    loads[2].wait()
    loads[3].wait()
    gain = jnp.concatenate([gain_ref[i : i + 1, :] for i in range(gain_ref.shape[0])], axis=1)
    floats = tokens[...].astype(f32)
    normed = (
        floats
        * lax.rsqrt(jnp.mean(floats * floats, axis=-1, keepdims=True) + norm_eps)
        * gain
    ).astype(bf16)
    loads[4].wait()
    raw = dot(normed, wq[...])
    query = jnp.concatenate(
        [rotate(raw[:, h * width : (h + 1) * width]) for h in range(local_heads)], axis=1
    ).astype(bf16)
    q_out[...] = dot(routed, query).reshape(n_dp, capacity, local_heads * width).astype(bf16)

    pl.semaphore_wait(barrier, n_all - 1)

    def remote(src, dst, k, where):
        return pltpu.make_async_remote_copy(
            src_ref=src,
            dst_ref=dst,
            send_sem=send_sem.at[k],
            recv_sem=recv_sem.at[k],
            device_id=where,
            device_id_type=MESH,
        )

    def local_copy(src, dst, k):
        return pltpu.make_async_copy(src, dst, recv_sem.at[k])

    def wait_for(ref, sem):
        pltpu.make_async_copy(ref, ref, sem).wait()

    @pl.loop(1, n_dp)
    def _(i):
        d = lax.rem(dp + i, n_dp)
        remote(meta_out.at[d], meta_in.at[dp], 0, (d, tp)).start()

    local_copy(meta_out.at[dp], meta_in.at[dp], 0).start()

    @pl.loop(1, n_all)
    def _(i):
        d, t = peer_of(i)
        remote(q_out.at[d], q_in.at[me], 1, (d, t)).start()

    local_copy(q_out.at[dp], q_in.at[me], 1).start()

    loads[6].wait()
    key_value = dot(normed, wkv[...])
    new_key = rotate(key_value[:, :width]).astype(bf16).astype(f32)
    new_value = key_value[:, width:].astype(bf16).astype(f32)
    self_scores = [
        jnp.sum(
            query[:, h * width : (h + 1) * width].astype(f32) * new_key, axis=1, keepdims=True
        )
        * scale
        for h in range(local_heads)
    ]

    loads[5].wait()
    table = table_ref[...].astype(f32)
    page_id = iota((pages, rows), 0).astype(f32)
    holds = [(page_id == table[j : j + 1, :]).astype(f32) for j in range(page_rows)]
    first_page = holds[0].astype(bf16)
    any_page = sum(holds).astype(bf16)
    which = sum(j * jnp.sum(holds[j], axis=1, keepdims=True) for j in range(page_rows))
    swap = dot_t(any_page, any_page)
    swap = jnp.where(iota((pages, pages), 0) == iota((pages, pages), 1), 0.0, swap)
    key_slot = (tp * page_rows * page_len).astype(f32) + which * page_len + iota(
        (pages, page_len), 1
    ).astype(f32)

    wait_for(meta_in, recv_sem.at[0])
    got = meta_in[...].astype(f32).reshape(slots, 128)
    serves = (got[:, 2:3] - 1.0 == iota((slots, rows), 1).astype(f32)).astype(bf16)
    to_page = dot_t(any_page, serves).astype(bf16)
    from_page = dot_t(serves, any_page).astype(bf16)
    from_first = dot_t(serves, first_page)
    page_meta = dot(to_page, got.astype(bf16))
    page_position = page_meta[:, 0:1] * 128.0 + page_meta[:, 1:2]
    gap = key_slot - page_position
    offset = gap - window * jnp.floor(gap * (1.0 / window))
    live = (offset != 0.0) & (page_position - window + offset >= 0.0)
    mask = jnp.where(live, 0.0, masked_score)

    wait_for(q_in, recv_sem.at[1])
    for t in range(n_tensor):
        part = q_in[t * n_dp : (t + 1) * n_dp].astype(f32).reshape(slots, local_heads * width)
        spread = dot(to_page, part.astype(bf16))
        for h in range(local_heads):
            page_q[pl.ds(t * local_heads + h, pages, stride=heads), :] = spread[
                :, h * width : (h + 1) * width
            ]

    for i in range(chunks):
        pool_load(i).wait()

    pairs = pages // 2
    unroll = 8

    @pl.loop(0, pairs // unroll)
    def _(step):
        for u in range(unroll):
            pair = step * unroll + u
            at = pl.multiple_of(pair * 2 * heads, 2 * heads)
            keys = pool[pl.ds(pair * 2, 2), :, :width].reshape(2 * page_len, width)
            scores = dot_t(page_q[pl.ds(at, 2 * heads), :].astype(bf16), keys)
            page_s[pl.ds(at, heads), :] = scores[:heads, :page_len]
            page_s[pl.ds(at + heads, heads), :] = scores[heads:, page_len:]

    lanes = lax.rem(iota((pages, 128), 1), heads)
    peaks = jnp.zeros((pages, 128), f32)
    for h in range(heads):
        scored = page_s[pl.ds(h, pages, stride=heads), :] * scale + mask
        top = jnp.max(scored, axis=1, keepdims=True)
        peaks = jnp.where(lanes == h, top, peaks)
    peaks = jnp.maximum(peaks, peak_floor)
    peaks = jnp.maximum(peaks, dot_exact(swap, peaks))
    totals = jnp.zeros((pages, 128), f32)
    for h in range(heads):
        scored = page_s[pl.ds(h, pages, stride=heads), :] * scale + mask
        weight = jnp.exp(scored - peaks[:, h : h + 1])
        totals = jnp.where(lanes == h, jnp.sum(weight, axis=1, keepdims=True), totals)
        page_s[pl.ds(h, pages, stride=heads), :] = weight

    upper = iota((2 * heads, page_len), 0) < heads

    @pl.loop(0, pairs // unroll)
    def _(step):
        for u in range(unroll):
            pair = step * unroll + u
            at = pl.multiple_of(pair * 2 * heads, 2 * heads)
            weight = page_s[pl.ds(at, 2 * heads), :]
            both = jnp.concatenate(
                [jnp.where(upper, weight, 0.0), jnp.where(upper, 0.0, weight)], axis=1
            ).astype(bf16)
            values = pool[pl.ds(pair * 2, 2), :, width:].reshape(2 * page_len, width)
            page_acc[pl.ds(at, 2 * heads), :] = dot(both, values)

    own_peak = split(dot_exact(from_first, peaks))
    own_total = split(dot_exact(from_page.astype(f32), totals))
    group = lax.div(iota((slots, 128), 1), heads)
    stats = jnp.zeros((slots, 128), f32)
    for k, piece in enumerate(own_peak + own_total):
        stats = jnp.where(group == k, piece, stats)
    stats = stats.reshape(n_dp, capacity, 128).astype(bf16)
    for t in range(n_tensor):
        for h in range(local_heads):
            summed = page_acc[pl.ds(t * local_heads + h, pages, stride=heads), :].astype(bf16)
            stat_out[t * n_dp : (t + 1) * n_dp, :, h * width : (h + 1) * width] = (
                dot(from_page, summed).reshape(n_dp, capacity, width).astype(bf16)
            )
        stat_out[t * n_dp : (t + 1) * n_dp, :, local_heads * width :] = stats

    @pl.loop(1, n_all)
    def _(i):
        d, t = peer_of(i)
        remote(stat_out.at[t * n_dp + d], stat_in.at[me], 2, (d, t)).start()

    local_copy(stat_out.at[me], stat_in.at[me], 2).start()

    loads[7].wait()
    wait_for(stat_in, recv_sem.at[2])
    parts = []
    for t in range(n_tensor):
        part = stat_in[t * n_dp : (t + 1) * n_dp].astype(f32).reshape(slots, stat_in.shape[2])
        parts.append(dot(from_place, part.astype(bf16)))
    row_lane = iota((rows, 128), 1)
    row_head = lax.rem(row_lane, heads)
    row_group = lax.div(row_lane, heads)
    attended = []
    for h in range(local_heads):
        mine = row_head == tp * local_heads + h
        is_peak = mine & (row_group < 3)
        is_total = mine & (row_group >= 3) & (row_group < 6)
        tops, sums = [], []
        for part in parts:
            stat = part[:, local_heads * width :]
            tops.append(jnp.sum(jnp.where(is_peak, stat, 0.0), axis=1, keepdims=True))
            sums.append(jnp.sum(jnp.where(is_total, stat, 0.0), axis=1, keepdims=True))
        overall = functools.reduce(jnp.maximum, tops, self_scores[h])
        fresh = jnp.exp(self_scores[h] - overall)
        total = fresh
        acc = fresh.astype(bf16).astype(f32) * new_value
        for top, add, part in zip(tops, sums, parts):
            keep = jnp.exp(top - overall)
            total = total + add * keep
            acc = acc + part[:, h * width : (h + 1) * width] * keep
        attended.append(acc / total)
    attended = jnp.concatenate(attended, axis=1).astype(bf16)
    partial = dot(attended, wo[...])
    sum_out[...] = partial.reshape(n_tensor, out_rows, partial.shape[1]).astype(bf16)

    @pl.loop(1, n_tensor)
    def _(i):
        t = lax.rem(tp + i, n_tensor)
        remote(sum_out.at[t], sum_in.at[tp], 3, (dp, t)).start()

    local_copy(sum_out.at[tp], sum_in.at[tp], 3).start()
    wait_for(sum_in, recv_sem.at[3])
    done = sum_in[0].astype(f32)
    for t in range(1, n_tensor):
        done = done + sum_in[t].astype(f32)
    out_ref[tp] = done.astype(bf16)

    @pl.loop(1, n_tensor)
    def _(i):
        t = lax.rem(tp + i, n_tensor)
        remote(out_ref.at[tp], out_ref.at[tp], 4, (dp, t)).start()

    wait_for(out_ref.at[pl.ds(0, n_tensor - 1)], recv_sem.at[4])
    wait_for(meta_in.at[pl.ds(0, n_dp - 1)], send_sem.at[0])
    wait_for(q_in.at[pl.ds(0, n_all - 1)], send_sem.at[1])
    wait_for(stat_in.at[pl.ds(0, n_all - 1)], send_sem.at[2])
    wait_for(sum_in.at[pl.ds(0, n_tensor - 1)], send_sem.at[3])
    wait_for(out_ref.at[pl.ds(0, n_tensor - 1)], send_sem.at[4])


def local(tokens, norm_gain, w_query, w_keyval, w_out, kv_pool, page_table, positions, assignment):
    n_dp, n_tensor = lax.axis_size("dp"), lax.axis_size("tensor")
    rows, model = tokens.shape
    width = w_keyval.shape[1] // 2
    query_width = w_query.shape[1]
    heads = query_width // width * n_tensor
    capacity = max(8, rows // n_dp)
    n_all = n_dp * n_tensor
    pages = kv_pool.shape[0]
    whole = pl.BlockSpec(memory_space=pltpu.VMEM)
    far = pl.BlockSpec(memory_space=pltpu.HBM)
    out = pl.pallas_call(
        functools.partial(kernel, n_dp, n_tensor, capacity),
        out_shape=jax.ShapeDtypeStruct((n_tensor, rows // n_tensor, model), bf16),
        in_specs=[far] * 9,
        out_specs=whole,
        scratch_shapes=[
            pltpu.VMEM(tokens.shape, bf16),
            pltpu.VMEM((model // 128, 128), f32),
            pltpu.VMEM(page_table.shape[::-1], jnp.int32),
            pltpu.VMEM((1, rows), jnp.int32),
            pltpu.VMEM((1, rows), jnp.int32),
            pltpu.VMEM(w_query.shape, bf16),
            pltpu.VMEM(w_keyval.shape, bf16),
            pltpu.VMEM(w_out.shape, bf16),
            pltpu.VMEM(kv_pool.shape, bf16),
            pltpu.VMEM((n_dp, capacity, query_width), bf16),
            pltpu.VMEM((n_dp, capacity, 128), bf16),
            pltpu.VMEM((n_all, capacity, query_width), bf16),
            pltpu.VMEM((n_dp, capacity, 128), bf16),
            pltpu.VMEM((pages * heads, width), f32),
            pltpu.VMEM((pages * heads, kv_pool.shape[1]), f32),
            pltpu.VMEM((pages * heads, width), f32),
            pltpu.VMEM((n_all, capacity, query_width + 128), bf16),
            pltpu.VMEM((n_all, capacity, query_width + 128), bf16),
            pltpu.VMEM((n_tensor, rows // n_tensor, model), bf16),
            pltpu.VMEM((n_tensor, rows // n_tensor, model), bf16),
            pltpu.SemaphoreType.DMA((8,)),
            pltpu.SemaphoreType.DMA((chunks,)),
            pltpu.SemaphoreType.DMA((5,)),
            pltpu.SemaphoreType.DMA((5,)),
        ],
        compiler_params=pltpu.CompilerParams(
            collective_id=0, has_side_effects=True, vmem_limit_bytes=62 << 20
        ),
    )(
        tokens,
        norm_gain.reshape(model // 128, 128),
        w_query,
        w_keyval,
        w_out,
        kv_pool,
        page_table.T,
        positions.reshape(1, rows),
        assignment.reshape(1, rows),
    )
    return out.reshape(rows, model)


def solution(mesh):
    return jax.shard_map(
        local,
        mesh=mesh,
        in_specs=(
            P("dp", None),
            P(),
            P(None, "tensor"),
            P(),
            P("tensor", None),
            P(("dp", "tensor"), None, None),
            P("dp", "tensor"),
            P("dp"),
            P("dp"),
        ),
        out_specs=P("dp", None),
        check_vma=False,
    )
```

```python
import functools
import math

import jax
import jax.numpy as jnp
from jax import lax
from jax.experimental import pallas as pl
from jax.experimental.pallas import tpu as pltpu
from jax.sharding import PartitionSpec as P

masked_score = -1e30
peak_floor = -1e29
norm_eps = 1e-06
rotary_base = 10000.0
chunks = 8
MESH = pl.DeviceIdType.MESH
f32 = jnp.float32
bf16 = jnp.bfloat16


def dot(a, b):
    return jnp.dot(a, b, preferred_element_type=f32)


def dot_t(a, b):
    return lax.dot_general(a, b, (((1,), (1,)), ((), ())), preferred_element_type=f32)


def dot_exact(a, b):
    return jnp.dot(a, b, preferred_element_type=f32, precision=lax.Precision.HIGHEST)


def iota(shape, axis):
    return lax.broadcasted_iota(jnp.int32, shape, axis)


def kernel(
    n_dp,
    n_tensor,
    capacity,
    tokens_hbm,
    gain_hbm,
    wq_hbm,
    wkv_hbm,
    wo_hbm,
    pool_hbm,
    table_hbm,
    position_hbm,
    assign_hbm,
    out_ref,
    tokens,
    gain_ref,
    table_ref,
    position_ref,
    assign_ref,
    wq,
    wkv,
    wo,
    pool,
    q_out,
    meta_out,
    q_in,
    meta_in,
    page_q,
    page_s,
    page_acc,
    stat_out,
    stat_in,
    small_out,
    small_in,
    sum_out,
    sum_in,
    pair_sum,
    load_sem,
    pool_sem,
    send_sem,
    recv_sem,
):
    dp = lax.axis_index("dp")
    tp = lax.axis_index("tensor")
    n_all = n_dp * n_tensor
    me = tp * n_dp + dp
    rows = tokens.shape[0]
    slots = n_dp * capacity
    width = wkv.shape[1] // 2
    half = width // 2
    local_heads = wq.shape[1] // width
    heads = local_heads * n_tensor
    pages, page_len = pool.shape[0], pool.shape[1]
    page_rows = table_ref.shape[0]
    window = page_rows * n_tensor * page_len
    chunk = pages // chunks
    scale = width ** (-0.5)
    out_rows = rows // n_tensor

    loads = [
        pltpu.make_async_copy(src, dst, load_sem.at[i])
        for i, (src, dst) in enumerate(
            (
                (position_hbm, position_ref),
                (assign_hbm, assign_ref),
                (tokens_hbm, tokens),
                (gain_hbm, gain_ref),
                (wq_hbm, wq),
                (table_hbm, table_ref),
                (wkv_hbm, wkv),
                (wo_hbm, wo),
            )
        )
    ]
    for load in loads[:5]:
        load.start()

    barrier = pltpu.get_barrier_semaphore()

    def peer_of(i):
        other = lax.rem(me + i, n_all)
        return lax.rem(other, n_dp), lax.div(other, n_dp)

    @pl.loop(1, n_all)
    def _(i):
        pl.semaphore_signal(barrier, inc=1, device_id=peer_of(i), device_id_type=MESH)

    for load in loads[5:]:
        load.start()

    def pool_load(i):
        part = pl.ds(i * chunk, chunk)
        return pltpu.make_async_copy(pool_hbm.at[part], pool.at[part], pool_sem.at[i])

    for i in range(chunks):
        pool_load(i).start()

    eye = iota((rows, rows), 0) == iota((rows, rows), 1)
    before = iota((rows, rows), 1) < iota((rows, rows), 0)
    after = iota((rows, rows), 1) > iota((rows, rows), 0)

    def as_column(row):
        return jnp.sum(jnp.where(eye, row, 0.0), axis=1, keepdims=True)

    loads[0].wait()
    loads[1].wait()
    position_row = position_ref[...].astype(f32)
    position = as_column(position_row)
    target_int = lax.div(assign_ref[...], rows)
    slot_row = (assign_ref[...] - target_int * rows).astype(f32)
    target_row = target_int.astype(f32)
    target = as_column(target_row)
    same = (target == target_row).astype(f32)
    place_row = target_row * capacity + jnp.sum(
        jnp.where(after, same, 0.0), axis=0, keepdims=True
    )
    place = target * capacity + jnp.sum(jnp.where(before, same, 0.0), axis=1, keepdims=True)
    to_place = iota((slots, rows), 0).astype(f32) == place_row
    from_place = (iota((rows, slots), 1).astype(f32) == place).astype(bf16)
    routed = to_place.astype(bf16)
    sent_position = jnp.sum(jnp.where(to_place, position_row, 0.0), axis=1, keepdims=True)
    sent_slot = jnp.sum(jnp.where(to_place, slot_row + 1.0, 0.0), axis=1, keepdims=True)
    high = jnp.floor(sent_position * (1.0 / 128.0))
    low = sent_position - high * 128.0
    lane = iota((slots, 128), 1)
    meta = jnp.where(lane == 0, high, jnp.where(lane == 1, low, jnp.where(lane == 2, sent_slot, 0.0)))
    meta_out[...] = meta.reshape(n_dp, capacity, 128).astype(bf16)

    step = -2.0 * math.log(rotary_base) / width
    angles = position * jnp.exp(iota((1, half), 1).astype(f32) * step)
    cosine = jnp.cos(angles)
    sine = jnp.sin(angles)

    def rotate(values):
        first, second = values[:, :half], values[:, half:]
        return jnp.concatenate(
            [first * cosine - second * sine, first * sine + second * cosine], axis=1
        )

    loads[2].wait()
    loads[3].wait()
    gain = jnp.concatenate([gain_ref[i : i + 1, :] for i in range(gain_ref.shape[0])], axis=1)
    floats = tokens[...].astype(f32)
    normed = (
        floats
        * lax.rsqrt(jnp.mean(floats * floats, axis=-1, keepdims=True) + norm_eps)
        * gain
    ).astype(bf16)
    loads[4].wait()
    raw = dot(normed, wq[...])
    query = jnp.concatenate(
        [rotate(raw[:, h * width : (h + 1) * width]) for h in range(local_heads)], axis=1
    ).astype(bf16)
    q_out[...] = dot(routed, query).reshape(n_dp, capacity, local_heads * width).astype(bf16)

    pl.semaphore_wait(barrier, n_all - 1)

    def remote(src, dst, k, where):
        return pltpu.make_async_remote_copy(
            src_ref=src,
            dst_ref=dst,
            send_sem=send_sem.at[k],
            recv_sem=recv_sem.at[k],
            device_id=where,
            device_id_type=MESH,
        )

    def local_copy(src, dst, k):
        return pltpu.make_async_copy(src, dst, recv_sem.at[k])

    def wait_for(ref, sem):
        pltpu.make_async_copy(ref, ref, sem).wait()

    @pl.loop(1, n_dp)
    def _(i):
        d = lax.rem(dp + i, n_dp)
        remote(meta_out.at[d], meta_in.at[dp], 0, (d, tp)).start()

    local_copy(meta_out.at[dp], meta_in.at[dp], 0).start()

    @pl.loop(1, n_all)
    def _(i):
        d, t = peer_of(i)
        remote(q_out.at[d], q_in.at[me], 1, (d, t)).start()

    local_copy(q_out.at[dp], q_in.at[me], 1).start()

    loads[6].wait()
    key_value = dot(normed, wkv[...])
    new_key = rotate(key_value[:, :width]).astype(bf16).astype(f32)
    new_value = key_value[:, width:].astype(bf16).astype(f32)
    self_scores = [
        jnp.sum(
            query[:, h * width : (h + 1) * width].astype(f32) * new_key, axis=1, keepdims=True
        )
        * scale
        for h in range(local_heads)
    ]

    loads[5].wait()
    table = table_ref[...].astype(f32)
    page_id = iota((pages, rows), 0).astype(f32)
    holds = [(page_id == table[j : j + 1, :]).astype(f32) for j in range(page_rows)]
    first_page = holds[0].astype(bf16)
    any_page = sum(holds).astype(bf16)
    which = sum(j * jnp.sum(holds[j], axis=1, keepdims=True) for j in range(page_rows))
    swap = dot_t(any_page, any_page)
    swap = jnp.where(iota((pages, pages), 0) == iota((pages, pages), 1), 0.0, swap)
    key_slot = (tp * page_rows * page_len).astype(f32) + which * page_len + iota(
        (pages, page_len), 1
    ).astype(f32)

    wait_for(meta_in, recv_sem.at[0])
    got = meta_in[...].astype(f32).reshape(slots, 128)
    serves = (got[:, 2:3] - 1.0 == iota((slots, rows), 1).astype(f32)).astype(bf16)
    to_page = dot_t(any_page, serves).astype(bf16)
    from_page = dot_t(serves, any_page).astype(bf16)
    from_first = dot_t(serves, first_page)
    page_meta = dot(to_page, got.astype(bf16))
    page_position = page_meta[:, 0:1] * 128.0 + page_meta[:, 1:2]
    gap = key_slot - page_position
    offset = gap - window * jnp.floor(gap * (1.0 / window))
    live = (offset != 0.0) & (page_position - window + offset >= 0.0)
    mask = jnp.where(live, 0.0, masked_score)

    wait_for(q_in, recv_sem.at[1])
    for t in range(n_tensor):
        part = q_in[t * n_dp : (t + 1) * n_dp].astype(f32).reshape(slots, local_heads * width)
        spread = dot(to_page, part.astype(bf16))
        for h in range(local_heads):
            page_q[pl.ds(t * local_heads + h, pages, stride=heads), :] = spread[
                :, h * width : (h + 1) * width
            ]

    for i in range(chunks):
        pool_load(i).wait()

    pairs = pages // 2
    unroll = 8

    @pl.loop(0, pairs // unroll)
    def _(step):
        for u in range(unroll):
            pair = step * unroll + u
            at = pl.multiple_of(pair * 2 * heads, 2 * heads)
            keys = pool[pl.ds(pair * 2, 2), :, :width].reshape(2 * page_len, width)
            scores = dot_t(page_q[pl.ds(at, 2 * heads), :].astype(bf16), keys)
            page_s[pl.ds(at, heads), :] = scores[:heads, :page_len]
            page_s[pl.ds(at + heads, heads), :] = scores[heads:, page_len:]

    lanes = lax.rem(iota((pages, 128), 1), heads)
    peaks = jnp.zeros((pages, 128), f32)
    for h in range(heads):
        scored = page_s[pl.ds(h, pages, stride=heads), :] * scale + mask
        top = jnp.max(scored, axis=1, keepdims=True)
        peaks = jnp.where(lanes == h, top, peaks)
    peaks = jnp.maximum(peaks, peak_floor)
    peaks = jnp.maximum(peaks, dot_exact(swap, peaks))
    totals = jnp.zeros((pages, 128), f32)
    for h in range(heads):
        scored = page_s[pl.ds(h, pages, stride=heads), :] * scale + mask
        weight = jnp.exp(scored - peaks[:, h : h + 1])
        totals = jnp.where(lanes == h, jnp.sum(weight, axis=1, keepdims=True), totals)
        page_s[pl.ds(h, pages, stride=heads), :] = weight

    upper = iota((2 * heads, page_len), 0) < heads

    @pl.loop(0, pairs // unroll)
    def _(step):
        for u in range(unroll):
            pair = step * unroll + u
            at = pl.multiple_of(pair * 2 * heads, 2 * heads)
            weight = page_s[pl.ds(at, 2 * heads), :]
            both = jnp.concatenate(
                [jnp.where(upper, weight, 0.0), jnp.where(upper, 0.0, weight)], axis=1
            ).astype(bf16)
            values = pool[pl.ds(pair * 2, 2), :, width:].reshape(2 * page_len, width)
            page_acc[pl.ds(at, 2 * heads), :] = dot(both, values)

    own_peak = dot_exact(from_first, peaks)
    own_total = dot_exact(from_page.astype(f32), totals)
    packed = lax.div(iota((slots, 128), 1), heads)
    within = lax.rem(iota((slots, 128), 0), capacity)
    stats = jnp.where(
        packed == within, own_peak, jnp.where(packed == within + capacity, own_total, 0.0)
    )
    small_out[...] = jnp.sum(stats.reshape(n_dp, capacity, 128), axis=1, keepdims=True)
    for t in range(n_tensor):
        for h in range(local_heads):
            summed = page_acc[pl.ds(t * local_heads + h, pages, stride=heads), :].astype(bf16)
            stat_out[t * n_dp : (t + 1) * n_dp, :, h * width : (h + 1) * width] = (
                dot(from_page, summed).reshape(n_dp, capacity, width).astype(bf16)
            )

    @pl.loop(1, n_all)
    def _(i):
        d, t = peer_of(i)
        remote(small_out.at[d], small_in.at[me], 5, (d, t)).start()
        remote(stat_out.at[t * n_dp + d], stat_in.at[me], 2, (d, t)).start()

    local_copy(small_out.at[dp], small_in.at[me], 5).start()
    local_copy(stat_out.at[me], stat_in.at[me], 2).start()

    loads[7].wait()
    wait_for(stat_in, recv_sem.at[2])
    wait_for(small_in, recv_sem.at[5])
    parts, heads_of = [], []
    row_lane = iota((slots, 128), 1)
    row_head = lax.rem(row_lane, heads)
    row_place = lax.div(row_lane, heads)
    row_within = lax.rem(iota((slots, 128), 0), capacity)
    for t in range(n_tensor):
        part = stat_in[t * n_dp : (t + 1) * n_dp].astype(f32).reshape(slots, local_heads * width)
        parts.append(dot(from_place, part.astype(bf16)))
        small = jnp.broadcast_to(
            small_in[t * n_dp : (t + 1) * n_dp], (n_dp, capacity, 128)
        ).reshape(slots, 128)
        columns = jnp.zeros((slots, 128), f32)
        for h in range(local_heads):
            mine = row_head == tp * local_heads + h
            for k, at in enumerate((row_within, row_within + capacity)):
                picked = jnp.sum(
                    jnp.where(mine & (row_place == at), small, 0.0), axis=1, keepdims=True
                )
                columns = jnp.where(row_lane == 2 * h + k, picked, columns)
        heads_of.append(dot_exact(from_place.astype(f32), columns))
    attended = []
    for h in range(local_heads):
        tops = [column[:, 2 * h : 2 * h + 1] for column in heads_of]
        sums = [column[:, 2 * h + 1 : 2 * h + 2] for column in heads_of]
        overall = functools.reduce(jnp.maximum, tops, self_scores[h])
        fresh = jnp.exp(self_scores[h] - overall)
        total = fresh
        acc = fresh.astype(bf16).astype(f32) * new_value
        for top, add, part in zip(tops, sums, parts):
            keep = jnp.exp(top - overall)
            total = total + add * keep
            acc = acc + part[:, h * width : (h + 1) * width] * keep
        attended.append(acc / total)
    attended = jnp.concatenate(attended, axis=1).astype(bf16)
    partial = dot(attended, wo[...])
    sum_out[...] = partial.reshape(n_tensor, out_rows, partial.shape[1]).astype(bf16)

    parity = lax.rem(tp, 2)
    sibling = tp + 1 - 2 * parity
    opposite = lax.rem(tp + 2, n_tensor)
    mine = pl.ds(2 * parity, 2)
    theirs = pl.ds(2 - 2 * parity, 2)
    remote(sum_out.at[theirs], sum_in.at[0:2], 3, (dp, sibling)).start()
    wait_for(sum_in.at[0:2], recv_sem.at[3])
    pair_sum[...] = (sum_out[mine].astype(f32) + sum_in[0:2].astype(f32)).astype(bf16)
    remote(pair_sum, sum_in.at[2:4], 4, (dp, opposite)).start()
    wait_for(sum_in.at[2:4], recv_sem.at[4])
    out_ref[mine] = (pair_sum[...].astype(f32) + sum_in[2:4].astype(f32)).astype(bf16)
    remote(out_ref.at[mine], out_ref.at[mine], 6, (dp, sibling)).start()
    wait_for(out_ref.at[theirs], recv_sem.at[6])
    wait_for(meta_in.at[pl.ds(0, n_dp - 1)], send_sem.at[0])
    wait_for(q_in.at[pl.ds(0, n_all - 1)], send_sem.at[1])
    wait_for(stat_in.at[pl.ds(0, n_all - 1)], send_sem.at[2])
    wait_for(small_in.at[pl.ds(0, n_all - 1)], send_sem.at[5])
    for k in (3, 4, 6):
        wait_for(pair_sum, send_sem.at[k])


def local(tokens, norm_gain, w_query, w_keyval, w_out, kv_pool, page_table, positions, assignment):
    n_dp, n_tensor = lax.axis_size("dp"), lax.axis_size("tensor")
    rows, model = tokens.shape
    width = w_keyval.shape[1] // 2
    query_width = w_query.shape[1]
    heads = query_width // width * n_tensor
    capacity = max(8, rows // n_dp)
    n_all = n_dp * n_tensor
    pages = kv_pool.shape[0]
    whole = pl.BlockSpec(memory_space=pltpu.VMEM)
    far = pl.BlockSpec(memory_space=pltpu.HBM)
    out = pl.pallas_call(
        functools.partial(kernel, n_dp, n_tensor, capacity),
        out_shape=jax.ShapeDtypeStruct((n_tensor, rows // n_tensor, model), bf16),
        in_specs=[far] * 9,
        out_specs=whole,
        scratch_shapes=[
            pltpu.VMEM(tokens.shape, bf16),
            pltpu.VMEM((model // 128, 128), f32),
            pltpu.VMEM(page_table.shape[::-1], jnp.int32),
            pltpu.VMEM((1, rows), jnp.int32),
            pltpu.VMEM((1, rows), jnp.int32),
            pltpu.VMEM(w_query.shape, bf16),
            pltpu.VMEM(w_keyval.shape, bf16),
            pltpu.VMEM(w_out.shape, bf16),
            pltpu.VMEM(kv_pool.shape, bf16),
            pltpu.VMEM((n_dp, capacity, query_width), bf16),
            pltpu.VMEM((n_dp, capacity, 128), bf16),
            pltpu.VMEM((n_all, capacity, query_width), bf16),
            pltpu.VMEM((n_dp, capacity, 128), bf16),
            pltpu.VMEM((pages * heads, width), f32),
            pltpu.VMEM((pages * heads, kv_pool.shape[1]), f32),
            pltpu.VMEM((pages * heads, width), f32),
            pltpu.VMEM((n_all, capacity, query_width), bf16),
            pltpu.VMEM((n_all, capacity, query_width), bf16),
            pltpu.VMEM((n_dp, 1, 128), f32),
            pltpu.VMEM((n_all, 1, 128), f32),
            pltpu.VMEM((n_tensor, rows // n_tensor, model), bf16),
            pltpu.VMEM((n_tensor, rows // n_tensor, model), bf16),
            pltpu.VMEM((2, rows // n_tensor, model), bf16),
            pltpu.SemaphoreType.DMA((8,)),
            pltpu.SemaphoreType.DMA((chunks,)),
            pltpu.SemaphoreType.DMA((7,)),
            pltpu.SemaphoreType.DMA((7,)),
        ],
        compiler_params=pltpu.CompilerParams(
            collective_id=0, has_side_effects=True, vmem_limit_bytes=62 << 20
        ),
    )(
        tokens,
        norm_gain.reshape(model // 128, 128),
        w_query,
        w_keyval,
        w_out,
        kv_pool,
        page_table.T,
        positions.reshape(1, rows),
        assignment.reshape(1, rows),
    )
    return out.reshape(rows, model)


def solution(mesh):
    return jax.shard_map(
        local,
        mesh=mesh,
        in_specs=(
            P("dp", None),
            P(),
            P(None, "tensor"),
            P(),
            P("tensor", None),
            P(("dp", "tensor"), None, None),
            P("dp", "tensor"),
            P("dp"),
            P("dp"),
        ),
        out_specs=P("dp", None),
        check_vma=False,
    )
```
